32 devices in a mesh: tm: 4 (over x, core), rows: 8 (over z, y).
Axes of the slice: x: 2, y: 2, z: 4, core: 2. Of those that a mesh axis runs over, the one named last changes fastest.
Arguments:
- features: bfloat16 [8, 16, 128, 384], P('tm', 'rows'), may hold values from -6 to 6
- block_gain: float32 [384], replicated, may hold values from 0.5 to 1.5
- conv_weight: bfloat16 [3, 3, 3, 384, 384], replicated, may hold values from -0.0625 to 0.0625
- conv_bias: float32 [384], replicated, may hold values from -3 to 3
- latent_weight: bfloat16 [384, 16], replicated, may hold values from -0.3125 to 0.3125
- latent_bias: float32 [16], replicated, may hold values from -3 to 3
- patch_weight: bfloat16 [64, 5120], replicated, may hold values from -0.75 to 0.75
- patch_bias: float32 [5120], replicated, may hold values from -3 to 3
- shift_mod: float32 [5120], replicated, may hold values from -4 to 4
- scale_mod: float32 [5120], replicated, may hold values from -2 to 2
- query_weight: bfloat16 [5120, 5120], P(None, 'tm'), may hold values from -0.078125 to 0.078125
- query_bias: float32 [5120], P('tm'), may hold values from -4 to 4
- query_gain: float32 [5120], P('tm'), may hold values from 0.5 to 1.5
- key_weight: bfloat16 [5120, 5120], P(None, 'tm'), may hold values from -0.078125 to 0.078125
- key_bias: float32 [5120], P('tm'), may hold values from -4 to 4
- key_gain: float32 [5120], P('tm'), may hold values from 0.5 to 1.5
- packing: int32 [32], replicated, may hold values from 0 to 31, each once
Outputs:
- queries: bfloat16 [4096, 5120], P('rows', 'tm')
- keys: bfloat16 [4096, 5120], P('rows', 'tm')
The draws below stay inside these ranges and needn't reach their ends.
All inputs are finite; a program needn't handle non-finite values.
Results may differ from the reference program's by a relative error of at most 0.0054.
Values may be sent and summed in bfloat16 or wider, within the bound.
A program may use at most 128 MiB of HBM per device.

```python
import jax
import jax.numpy as jnp
from jax import lax

C = 384
LAT = 16
D = 5120
FR_DEV = 2
ROW_DEV = 2
COLS = 128
TOK_DEV = 128
FRAMES = 8
ROWS_ALL = 16
BLOCKS = 32
TOKENS = 4096
N_TM = 4
N_ROWS = 8


def level_of(own_key, shape, shards, smallest, top_value):
    level, own = 1.0, jax.random.fold_in(own_key, 6)
    for axis_at, parts in shards:
        heights = jnp.exp(jax.random.uniform(jax.random.fold_in(own, axis_at), (parts,), jnp.float32, smallest / len(shards), top_value / len(shards)))
        level = level * jnp.repeat(heights, shape[axis_at] // parts).reshape([-1 if axis == axis_at else 1 for axis in range(len(shape))])
    return level


def noise(rng, extent, deviation, limit, cuts=(), kind=jnp.bfloat16):
    values = deviation * jax.random.normal(rng, extent, jnp.float32)
    if cuts:
        values = values * level_of(rng, extent, cuts, -0.22, 0.18)
    return jnp.clip(values, -limit, limit).astype(kind)


def setup_inputs(seed: int = 0) -> dict:
    seeds = jax.random.split(jax.random.key(seed), 18)
    return {
        "features": noise(seeds[0], (FRAMES, ROWS_ALL, COLS, C), 1.0, 6.0, ((0, 4), (1, 8))),
        "block_gain": jnp.clip(jax.random.uniform(seeds[1], (C,), jnp.float32, 0.5, 1.5), 0.5, 1.5),
        "conv_weight": noise(seeds[2], (3, 3, 3, C, C), (27 * C) ** -0.5, 0.0625),
        "conv_bias": noise(seeds[3], (C,), 0.5, 3.0, (), jnp.float32),
        "latent_weight": noise(seeds[4], (C, LAT), C ** -0.5, 0.3125),
        "latent_bias": noise(seeds[5], (LAT,), 0.5, 3.0, (), jnp.float32),
        "patch_weight": noise(seeds[6], (4 * LAT, D), (4 * LAT) ** -0.5, 0.75),
        "patch_bias": noise(seeds[7], (D,), 0.5, 3.0, (), jnp.float32),
        "shift_mod": noise(seeds[8], (D,), 1.0, 4.0, (), jnp.float32),
        "scale_mod": noise(seeds[9], (D,), 0.5, 2.0, (), jnp.float32),
        "query_weight": noise(seeds[10], (D, D), D ** -0.5, 0.078125, ((1, 4),)),
        "query_bias": noise(seeds[11], (D,), 1.0, 4.0, ((0, 4),), jnp.float32),
        "query_gain": jnp.clip(0.5 + 1.0 * jax.random.uniform(seeds[12], (D,), jnp.float32) ** level_of(seeds[12], (D,), ((0, 4),), -0.2, 0.2), 0.5, 1.5),
        "key_weight": noise(seeds[13], (D, D), D ** -0.5, 0.078125, ((1, 4),)),
        "key_bias": noise(seeds[14], (D,), 1.0, 4.0, ((0, 4),), jnp.float32),
        "key_gain": jnp.clip(0.5 + 1.0 * jax.random.uniform(seeds[15], (D,), jnp.float32) ** level_of(seeds[15], (D,), ((0, 4),), -0.2, 0.2), 0.5, 1.5),
        "packing": jax.random.permutation(seeds[16], BLOCKS).astype(jnp.int32),
    }


epsilon = 1e-06

def normed_act(features, block_gain):
    values = features.astype(jnp.float32)
    square_mean = lax.optimization_barrier(jnp.mean(values * values, axis=-1, keepdims=True))
    return jax.nn.silu(values * lax.rsqrt(square_mean + epsilon) * block_gain).astype(jnp.bfloat16)

def causal_conv(padded, conv_weight, frames, rows_count, cols_count, channels):
    total = jnp.zeros((frames * rows_count * cols_count, channels), jnp.float32)
    for depth_at in range(3):
        for row_at in range(3):
            slab_part = padded[depth_at:depth_at + frames, row_at:row_at + rows_count]
            joined = jnp.concatenate([slab_part[:, :, 0:cols_count], slab_part[:, :, 1:cols_count + 1], slab_part[:, :, 2:cols_count + 2]], axis=-1)
            kernel = conv_weight[depth_at, row_at].reshape(3 * channels, channels)
            total = total + jnp.dot(joined.reshape(-1, 3 * channels), kernel, preferred_element_type=jnp.float32)
    return total.reshape(frames, rows_count, cols_count, channels)

def project_norm(modulated, weight, bias, gain):
    values = jnp.dot(modulated, weight, preferred_element_type=jnp.float32) + bias
    square_mean = lax.optimization_barrier(jnp.mean(values * values, axis=-1, keepdims=True))
    return (values * lax.rsqrt(square_mean + epsilon) * gain).astype(jnp.bfloat16)

def reference(features, block_gain, conv_weight, conv_bias, latent_weight, latent_bias, patch_weight, patch_bias, shift_mod, scale_mod, query_weight, query_bias, query_gain, key_weight, key_bias, key_gain, packing):
    act = normed_act(features, block_gain)
    padded = jnp.pad(act, ((2, 0), (1, 1), (1, 1), (0, 0)))
    conv = causal_conv(padded, conv_weight, FRAMES, ROWS_ALL, COLS, C)
    block_out = (features.astype(jnp.float32) + conv + conv_bias).astype(jnp.bfloat16)
    latent = (jnp.dot(block_out.reshape(-1, C), latent_weight, preferred_element_type=jnp.float32) + latent_bias).astype(jnp.bfloat16)
    latent = latent.reshape(N_TM, FR_DEV, N_ROWS, ROW_DEV // 2, 2, COLS // 2, 2, LAT)
    blocks = jnp.transpose(latent, (0, 2, 7, 4, 6, 1, 3, 5)).reshape(BLOCKS, 4 * LAT, TOK_DEV)
    chosen = jnp.take(blocks, packing.astype(jnp.int32), axis=0)
    packed = jnp.transpose(chosen, (0, 2, 1)).reshape(TOKENS, 4 * LAT)
    embedded = jnp.dot(packed, patch_weight, preferred_element_type=jnp.float32) + patch_bias
    center = lax.optimization_barrier(jnp.mean(embedded, axis=-1, keepdims=True))
    spread = lax.optimization_barrier(jnp.mean((embedded - center) ** 2, axis=-1, keepdims=True))
    modulated = ((embedded - center) * lax.rsqrt(spread + epsilon) * (1.0 + scale_mod) + shift_mod).astype(jnp.bfloat16)
    queries = project_norm(modulated, query_weight, query_bias, query_gain)
    keys = project_norm(modulated, key_weight, key_bias, key_gain)
    return (queries, keys)
```

```python
import functools

import jax
import jax.numpy as jnp
from jax import lax
from jax.experimental import pallas as pl
from jax.experimental.pallas import tpu as pltpu
from jax.sharding import PartitionSpec as P

epsilon = 1e-06
MESH = pl.DeviceIdType.MESH
F32, BF16 = jnp.float32, jnp.bfloat16
HIGH = lax.Precision.HIGHEST


def dot(a, b, **kw):
    return jnp.dot(a, b, preferred_element_type=F32, **kw)


def kernel(
    count_t, count_r,
    packing, feat_h, gain_h, conv_h, cbias_h, lw_h, lbias_h, pw_h, pb_h, shift_h, scale_h,
    wq_h, qb_h, qg_h, wk_h, kb_h, kg_h,
    q_out, k_out,
    feat, gain, conv, cbias, lw, lbias, pw, pb, shift, scale, wq, qb, qg, wk, kb, kg,
    rb, km, lhs, y_ref, fold, snd, rcv, tot, lat_all, emb, mod, qf, kf, sq_q, sq_k, sums_s, sums_r,
    lsem, wsem, hs_sem, hr_sem, as_sem, ar_sem, ss_sem, sr_sem,
):
    t, r = lax.axis_index("tm"), lax.axis_index("rows")
    count = count_t * count_r
    own = t * count_r + r
    _, _, cols, chans = feat.shape
    width = emb.shape[1]
    half = cols // 2
    feats = pw_h.shape[0]
    tokens = mod.shape[0]
    per_block = 2 * half

    small = [(feat_h, feat), (gain_h, gain), (lw_h, lw), (cbias_h, cbias), (lbias_h, lbias)]
    late = [
        (pw_h, pw.at[pl.ds(0, feats)]), (pw_h, pw.at[pl.ds(feats, feats)]), (pb_h, pb), (shift_h, shift),
        (scale_h, scale), (qb_h, qb), (qg_h, qg), (kb_h, kb), (kg_h, kg),
    ]
    copies = [pltpu.make_async_copy(s, d, lsem.at[i]) for i, (s, d) in enumerate(small + late)]
    early, later = copies[: len(small)], copies[len(small) :]
    for c in early:
        c.start()
    conv_copies = [pltpu.make_async_copy(conv_h.at[:, b], conv.at[:, b], wsem.at[b]) for b in range(3)]
    for c in conv_copies:
        c.start()
    for c in later:
        c.start()
    wq_copy = pltpu.make_async_copy(wq_h, wq, wsem.at[3])
    wk_copy = pltpu.make_async_copy(wk_h, wk, wsem.at[4])

    barrier = pltpu.get_barrier_semaphore()

    def greet(i, c):
        other = lax.rem(own + i, count)
        pl.semaphore_signal(barrier, inc=1, device_id=(other // count_r, lax.rem(other, count_r)), device_id_type=MESH)
        return c

    lax.fori_loop(1, count, greet, 0)

    for c in early:
        c.wait()

    lats = lw.shape[1]
    li = lax.broadcasted_iota(jnp.int32, (lats, 2 * feats), 0)
    lj = lax.broadcasted_iota(jnp.int32, (lats, 2 * feats), 1)
    both = ((lj % feats) // 4) == li
    e_both = jnp.where(both, 1.0, 0.0)
    e_low = jnp.where(both & (lj < feats), 1.0, 0.0)
    e_high = jnp.where(both & (lj >= feats), 1.0, 0.0)
    lwv = lw[...]
    lw_low = dot(lwv, e_low.astype(BF16)).astype(BF16)
    lw_high = dot(lwv, e_high.astype(BF16)).astype(BF16)
    lw_both = dot(lwv, e_both.astype(BF16)).astype(BF16)
    span = 2 * feats
    rb[...] = jnp.zeros(rb.shape, BF16)
    rb[pl.ds(0, chans), pl.ds(0, span)] = lw_low
    rb[pl.ds(chans, chans), pl.ds(0, span)] = lw_high
    rb[pl.ds(2 * chans, chans), pl.ds(span, span)] = lw_both
    km[pl.ds(3 * chans, chans), :] = jnp.zeros((chans, km.shape[1]), BF16)
    km[pl.ds(3 * chans, chans), pl.ds(2 * span, span)] = lw_low
    cb8 = jnp.broadcast_to(cbias[...].reshape(1, chans), (8, chans))
    lb8 = jnp.broadcast_to(lbias[...].reshape(1, lats), (8, lats))
    bias8 = dot(cb8, lw_both.astype(F32), precision=HIGH) + dot(lb8, e_both, precision=HIGH)

    gain_v = gain[...].reshape(1, chans)
    row_at = lax.broadcasted_iota(jnp.int32, (cols, chans), 0)
    for f in range(2):
        for w in range(2):
            raw = feat[f, w]
            v = raw.astype(F32)
            sm = jnp.mean(v * v, axis=-1, keepdims=True)
            x = v * lax.rsqrt(sm + epsilon) * gain_v
            act = (x / (1.0 + jnp.exp(-x))).astype(BF16)
            a32 = act.astype(F32)
            prev = jnp.where(row_at == 0, 0.0, pltpu.roll(a32, 1, 0))
            nxt = jnp.where(row_at == cols - 1, 0.0, pltpu.roll(a32, cols - 1, 0))
            at = pl.ds((f * 2 + w) * cols, cols)
            lhs[at, pl.ds(0, chans)] = prev.astype(BF16)
            lhs[at, pl.ds(chans, chans)] = act
            lhs[at, pl.ds(2 * chans, chans)] = nxt.astype(BF16)
            lhs[at, pl.ds(3 * chans, chans)] = raw

    rbv = rb[...]
    for b in range(3):
        conv_copies[b].wait()
        if b == 2:
            wq_copy.start()
            wk_copy.start()
        for e in range(3):
            w3 = jnp.concatenate([conv[2, b, e], conv[1, b, e], conv[0, b, e]], axis=1)
            km[pl.ds(e * chans, chans), pl.ds(b * 2 * span, 2 * span)] = dot(w3, rbv).astype(BF16)

    y_ref[...] = dot(lhs[...], km[...])

    lane = lax.broadcasted_iota(jnp.int32, (cols, span), 1)
    row = lax.broadcasted_iota(jnp.int32, (cols, span), 0)
    even_row = (lane & 2) == 0
    low = lane < feats
    parity = (lane & 1) == (row & 1)

    def y(f, w, b, z):
        return y_ref[pl.ds((f * 2 + w) * cols, cols), pl.ds(b * 2 * span + z * span, span)]

    def mid(f, z):
        return jnp.where(even_row, y(f, 0, 1, z) + y(f, 1, 2, z), y(f, 0, 0, z) + y(f, 1, 1, z))

    def up(f, z):
        return jnp.where(even_row, 0.0, y(f, 0, 2, z))

    def down(f, z):
        return jnp.where(even_row, y(f, 1, 0, z), 0.0)

    for i, part in enumerate((mid, up, down)):
        x0, x1 = part(0, 0), pltpu.roll(part(1, 0), feats, 1)
        mine = jnp.where(low, x0, x0 + x1)
        after = jnp.where(low, x1 + part(0, 1), part(1, 1))
        fold[i] = jnp.where(parity, mine, 0.0)
        fold[3 + i] = jnp.where(parity, after, 0.0)
    for i in range(6):
        snd[i] = fold[i, pl.ds(0, half, 2), :] + fold[i, pl.ds(1, half, 2), :]

    pl.semaphore_wait(barrier, count - 1)

    has_up, has_down = r > 0, r < count_r - 1
    has_next, has_prev = t < count_t - 1, t > 0
    plan = [
        (1, 0, t, r - 1, has_up, has_down),
        (2, 1, t, r + 1, has_down, has_up),
        (3, 2, t + 1, r, has_next, has_prev),
        (4, 3, t + 1, r - 1, has_next & has_up, has_prev & has_down),
        (5, 4, t + 1, r + 1, has_next & has_down, has_prev & has_up),
    ]
    halo = [
        pltpu.make_async_remote_copy(
            src_ref=snd.at[s], dst_ref=rcv.at[d], send_sem=hs_sem.at[d], recv_sem=hr_sem.at[d],
            device_id=(dt, dr), device_id_type=MESH,
        )
        for s, d, dt, dr, _, _ in plan
    ]
    for copy, (_, _, _, _, sends, _) in zip(halo, plan):
        pl.when(sends)(copy.start)
    tot[...] = snd[0] + bias8[0:1, :]
    for copy, (_, d, _, _, _, gets) in zip(halo, plan):
        def take(copy=copy, d=d):
            copy.wait_recv()
            tot[...] += rcv[d]
        pl.when(gets)(take)
    lat_all[own] = tot[...].astype(BF16)

    def to_all(i):
        other = lax.rem(own + i, count)
        return pltpu.make_async_remote_copy(
            src_ref=lat_all.at[own], dst_ref=lat_all.at[own], send_sem=as_sem.at[i], recv_sem=ar_sem.at[own],
            device_id=(other // count_r, lax.rem(other, count_r)), device_id_type=MESH,
        )

    def from_one(i):
        other = lax.rem(own + i, count)
        return pltpu.make_async_remote_copy(
            src_ref=lat_all.at[other], dst_ref=lat_all.at[other], send_sem=as_sem.at[i], recv_sem=ar_sem.at[other],
            device_id=(other // count_r, lax.rem(other, count_r)), device_id_type=MESH,
        )

    def send(i, c):
        to_all(i).start()
        return c

    lax.fori_loop(1, count, send, 0)
    for c in later:
        c.wait()

    def arrive(i, c):
        from_one(i).wait_recv()
        return c

    lax.fori_loop(1, count, arrive, 0)

    step = 512
    plane = lax.broadcasted_iota(jnp.int32, (half, span), 1)

    def lanes_sum(v):
        out = v[:, 0:128]
        for i in range(1, v.shape[1] // 128):
            out = out + v[:, i * 128 : (i + 1) * 128]
        return out

    def block(j, carry):
        p32 = lat_all[packing[r * count_t + j]].astype(F32)
        left = jnp.concatenate(
            [jnp.where(plane < feats, p32, 0.0), jnp.where(plane < feats, 0.0, p32)], axis=0
        ).astype(BF16)
        total = jnp.zeros((per_block, 128), F32)
        for c in range(0, width, step):
            e = dot(left, pw[:, c : c + step]) + pb[pl.ds(c, step)].reshape(1, step)
            emb[:, c : c + step] = e
            total = total + lanes_sum(e)
        center = jnp.sum(total, axis=1, keepdims=True) / width
        total = jnp.zeros((per_block, 128), F32)
        for c in range(0, width, step):
            d = emb[:, c : c + step] - center
            total = total + lanes_sum(d * d)
        inv = lax.rsqrt(jnp.sum(total, axis=1, keepdims=True) / width + epsilon)
        at = pl.ds(pl.multiple_of(j * per_block, per_block), per_block)
        for c in range(0, width, step):
            gains = 1.0 + scale[pl.ds(c, step)].reshape(1, step)
            moved = shift[pl.ds(c, step)].reshape(1, step)
            mod[at, c : c + step] = ((emb[:, c : c + step] - center) * inv * gains + moved).astype(BF16)
        return carry

    lax.fori_loop(0, count_t, block, 0)

    part = qf.shape[1]
    tile = 256 if part % 256 == 0 else 128
    for copy, w, bias, out, sq in ((wq_copy, wq, qb, qf, sq_q), (wk_copy, wk, kb, kf, sq_k)):
        copy.wait()
        sq[...] = jnp.zeros(sq.shape, F32)

        def project(n, carry, w=w, bias=bias, out=out, sq=sq):
            at = pl.ds(pl.multiple_of(n * tile, tile), tile)
            v = dot(mod[...], w[:, at]) + bias[at].reshape(1, tile)
            out[:, at] = v
            sq[...] += lanes_sum(v * v)
            return carry

        lax.fori_loop(0, part // tile, project, 0)

    ones = jnp.ones((4, 128), F32)
    nt = (((1,), (1,)), ((), ()))
    sums_s[...] = jnp.concatenate(
        [
            lax.dot_general(ones, sq_q[...], nt, precision=HIGH, preferred_element_type=F32),
            lax.dot_general(ones, sq_k[...], nt, precision=HIGH, preferred_element_type=F32),
        ],
        axis=0,
    )
    shares = [
        pltpu.make_async_remote_copy(
            src_ref=sums_s, dst_ref=sums_r.at[i - 1], send_sem=ss_sem.at[i - 1], recv_sem=sr_sem.at[i - 1],
            device_id=(lax.rem(t + i, count_t), r), device_id_type=MESH,
        )
        for i in range(1, count_t)
    ]
    for c in shares:
        c.start()
    sums = sums_s[...]
    for i, c in enumerate(shares):
        c.wait_recv()
        sums = sums + sums_r[i]
    inv = lax.rsqrt(sums / width + epsilon)
    pick = lax.broadcasted_iota(jnp.int32, (8, 128), 0)
    tn = (((0,), (0,)), ((), ()))
    inv_q = lax.dot_general(inv, jnp.where(pick == 0, 1.0, 0.0), tn, precision=HIGH, preferred_element_type=F32)
    inv_k = lax.dot_general(inv, jnp.where(pick == 4, 1.0, 0.0), tn, precision=HIGH, preferred_element_type=F32)
    for src, inv_v, gains, out in ((qf, inv_q, qg, q_out), (kf, inv_k, kg, k_out)):
        for c in range(0, part, 128):
            out[:, c : c + 128] = (src[:, c : c + 128] * inv_v * gains[pl.ds(c, 128)].reshape(1, 128)).astype(BF16)

    for copy, (_, _, _, _, sends, _) in zip(halo, plan):
        pl.when(sends)(copy.wait_send)

    def sent(i, c):
        to_all(i).wait_send()
        return c

    lax.fori_loop(1, count, sent, 0)
    for c in shares:
        c.wait_send()


def per_device(
    features, block_gain, conv_weight, conv_bias, latent_weight, latent_bias, patch_weight, patch_bias,
    shift_mod, scale_mod, query_weight, query_bias, query_gain, key_weight, key_bias, key_gain, packing,
):
    count_t, count_r = lax.axis_size("tm"), lax.axis_size("rows")
    count = count_t * count_r
    _, _, cols, chans = features.shape
    feats, width = patch_weight.shape
    part = query_weight.shape[1]
    half = cols // 2
    span = 2 * feats
    tokens = count_t * cols
    V = pltpu.VMEM
    operands = (
        packing, features, block_gain, conv_weight, conv_bias, latent_weight, latent_bias, patch_weight, patch_bias,
        shift_mod, scale_mod, query_weight, query_bias, query_gain, key_weight, key_bias, key_gain,
    )
    like = lambda a: V(a.shape, a.dtype)
    scratch = [like(a) for a in operands[1:7]]
    scratch += [V((2 * feats, width), BF16), like(patch_bias), like(shift_mod), like(scale_mod)]
    scratch += [like(a) for a in operands[11:]]
    scratch += [
        V((3 * chans, 2 * span), BF16),
        V((4 * chans, 6 * span), BF16),
        V((4 * cols, 4 * chans), BF16),
        V((4 * cols, 6 * span), F32),
        V((6, cols, span), F32),
        V((6, half, span), F32),
        V((5, half, span), F32),
        V((half, span), F32),
        V((count, half, span), BF16),
        V((cols, width), F32),
        V((tokens, width), BF16),
        V((tokens, part), F32),
        V((tokens, part), F32),
        V((tokens, 128), F32),
        V((tokens, 128), F32),
        V((8, tokens), F32),
        V((count_t - 1, 8, tokens), F32),
    ]
    dma = pltpu.SemaphoreType.DMA
    scratch += [dma((14,)), dma((5,)), dma((5,)), dma((5,)), dma((count,)), dma((count,)), dma((count_t - 1,)), dma((count_t - 1,))]
    out = jax.ShapeDtypeStruct((tokens, part), BF16)
    return pl.pallas_call(
        functools.partial(kernel, count_t, count_r),
        out_shape=(out, out),
        in_specs=[pl.BlockSpec(memory_space=pltpu.SMEM)] + [pl.BlockSpec(memory_space=pl.ANY)] * 16,
        out_specs=(pl.BlockSpec(memory_space=V),) * 2,
        scratch_shapes=scratch,
        compiler_params=pltpu.CompilerParams(collective_id=0, has_side_effects=True, vmem_limit_bytes=67043328),
    )(*operands)


def solution(mesh):
    in_specs = (
        P("tm", "rows", None, None), P(), P(), P(), P(), P(), P(), P(), P(), P(),
        P(None, "tm"), P("tm"), P("tm"), P(None, "tm"), P("tm"), P("tm"), P(),
    )
    out_specs = (P("rows", "tm"), P("rows", "tm"))
    return jax.shard_map(per_device, mesh=mesh, in_specs=in_specs, out_specs=out_specs, check_vma=False)
```

```python
import functools

import jax
import jax.numpy as jnp
from jax import lax
from jax.experimental import pallas as pl
from jax.experimental.pallas import tpu as pltpu
from jax.sharding import PartitionSpec as P

epsilon = 1e-06
MESH = pl.DeviceIdType.MESH
F32, BF16 = jnp.float32, jnp.bfloat16
HIGH = lax.Precision.HIGHEST


def dot(a, b, **kw):
    return jnp.dot(a, b, preferred_element_type=F32, **kw)


def kernel(
    count_t, count_r,
    packing, feat_h, gain_h, conv_h, cbias_h, lw_h, lbias_h, pw_h, pb_h, shift_h, scale_h,
    wq_h, qb_h, wk_h, kb_h,
    q_out, k_out, inv_out,
    feat, gain, conv, cbias, lw, lbias, pw, pb, shift, scale, wq, qb, wk, kb,
    rb, km, lhs, y_ref, fold, snd, rcv, tot, lat_all, emb, mod, qf, kf, sq, sums_s, sums_r,
    lsem, wsem, hs_sem, hr_sem, as_sem, ar_sem, ss_sem, sr_sem, osem,
):
    t, r = lax.axis_index("tm"), lax.axis_index("rows")
    count = count_t * count_r
    own = t * count_r + r
    _, _, cols, chans = feat.shape
    width = emb.shape[1]
    half = cols // 2
    feats = pw_h.shape[0]
    tokens = mod.shape[0]
    per_block = 2 * half

    small = [(feat_h, feat), (gain_h, gain), (lw_h, lw), (cbias_h, cbias), (lbias_h, lbias)]
    late = [
        (pw_h, pw.at[pl.ds(0, feats)]), (pw_h, pw.at[pl.ds(feats, feats)]), (pb_h, pb), (shift_h, shift),
        (scale_h, scale), (qb_h, qb), (kb_h, kb),
    ]
    copies = [pltpu.make_async_copy(s, d, lsem.at[i]) for i, (s, d) in enumerate(small + late)]
    early, later = copies[: len(small)], copies[len(small) :]
    for c in early:
        c.start()
    conv_copies = [pltpu.make_async_copy(conv_h.at[:, b], conv.at[:, b], wsem.at[b]) for b in range(3)]
    for c in conv_copies:
        c.start()
    for c in later:
        c.start()
    wq_copy = pltpu.make_async_copy(wq_h, wq, wsem.at[3])
    wk_copy = pltpu.make_async_copy(wk_h, wk, wsem.at[4])

    barrier = pltpu.get_barrier_semaphore()

    def greet(i, c):
        other = lax.rem(own + i, count)
        pl.semaphore_signal(barrier, inc=1, device_id=(other // count_r, lax.rem(other, count_r)), device_id_type=MESH)
        return c

    lax.fori_loop(1, count, greet, 0)

    for c in early:
        c.wait()

    lats = lw.shape[0]
    tn = (((0,), (0,)), ((), ()))
    li = lax.broadcasted_iota(jnp.int32, (lats, 2 * feats), 0)
    lj = lax.broadcasted_iota(jnp.int32, (lats, 2 * feats), 1)
    both = ((lj % feats) // 4) == li
    e_both = jnp.where(both, 1.0, 0.0)
    e_low = jnp.where(both & (lj < feats), 1.0, 0.0)
    e_high = jnp.where(both & (lj >= feats), 1.0, 0.0)
    lwv = lw[...]
    lw_low = lax.dot_general(lwv, e_low.astype(BF16), tn, preferred_element_type=F32).astype(BF16)
    lw_high = lax.dot_general(lwv, e_high.astype(BF16), tn, preferred_element_type=F32).astype(BF16)
    lw_both = lax.dot_general(lwv, e_both.astype(BF16), tn, preferred_element_type=F32).astype(BF16)
    span = 2 * feats
    rb[...] = jnp.zeros(rb.shape, BF16)
    rb[pl.ds(0, chans), pl.ds(0, span)] = lw_low
    rb[pl.ds(chans, chans), pl.ds(0, span)] = lw_high
    rb[pl.ds(2 * chans, chans), pl.ds(span, span)] = lw_both
    km[pl.ds(3 * chans, chans), :] = jnp.zeros((chans, km.shape[1]), BF16)
    km[pl.ds(3 * chans, chans), pl.ds(2 * span, span)] = lw_low
    cb8 = jnp.broadcast_to(cbias[...].reshape(1, chans), (8, chans))
    lb8 = jnp.broadcast_to(lbias[...].reshape(1, lats), (8, lats))
    bias8 = dot(cb8, lw_both.astype(F32), precision=HIGH) + dot(lb8, e_both, precision=HIGH)

    gain_v = gain[...].reshape(1, chans)
    row_at = lax.broadcasted_iota(jnp.int32, (cols, chans), 0)
    for f in range(2):
        for w in range(2):
            raw = feat[f, w]
            v = raw.astype(F32)
            sm = jnp.mean(v * v, axis=-1, keepdims=True)
            x = v * lax.rsqrt(sm + epsilon) * gain_v
            act = (x / (1.0 + jnp.exp(-x))).astype(BF16)
            a32 = act.astype(F32)
            prev = jnp.where(row_at == 0, 0.0, pltpu.roll(a32, 1, 0))
            nxt = jnp.where(row_at == cols - 1, 0.0, pltpu.roll(a32, cols - 1, 0))
            at = pl.ds((f * 2 + w) * cols, cols)
            lhs[at, pl.ds(0, chans)] = prev.astype(BF16)
            lhs[at, pl.ds(chans, chans)] = act
            lhs[at, pl.ds(2 * chans, chans)] = nxt.astype(BF16)
            lhs[at, pl.ds(3 * chans, chans)] = raw

    rbv = rb[...]
    for b in range(3):
        conv_copies[b].wait()
        if b == 2:
            wq_copy.start()
            wk_copy.start()
        for e in range(3):
            w3 = jnp.concatenate([conv[2, b, e], conv[1, b, e], conv[0, b, e]], axis=1)
            km[pl.ds(e * chans, chans), pl.ds(b * 2 * span, 2 * span)] = dot(w3, rbv).astype(BF16)

    y_ref[...] = dot(lhs[...], km[...])

    lane = lax.broadcasted_iota(jnp.int32, (cols, span), 1)
    row = lax.broadcasted_iota(jnp.int32, (cols, span), 0)
    even_row = (lane & 2) == 0
    low = lane < feats
    parity = (lane & 1) == (row & 1)

    def y(f, w, b, z):
        return y_ref[pl.ds((f * 2 + w) * cols, cols), pl.ds(b * 2 * span + z * span, span)]

    def mid(f, z):
        return jnp.where(even_row, y(f, 0, 1, z) + y(f, 1, 2, z), y(f, 0, 0, z) + y(f, 1, 1, z))

    def up(f, z):
        return jnp.where(even_row, 0.0, y(f, 0, 2, z))

    def down(f, z):
        return jnp.where(even_row, y(f, 1, 0, z), 0.0)

    for i, part in enumerate((mid, up, down)):
        x0, x1 = part(0, 0), pltpu.roll(part(1, 0), feats, 1)
        mine = jnp.where(low, x0, x0 + x1)
        after = jnp.where(low, x1 + part(0, 1), part(1, 1))
        fold[i] = jnp.where(parity, mine, 0.0)
        fold[3 + i] = jnp.where(parity, after, 0.0)
    for i in range(6):
        snd[i] = fold[i, pl.ds(0, half, 2), :] + fold[i, pl.ds(1, half, 2), :]

    pl.semaphore_wait(barrier, count - 1)

    has_up, has_down = r > 0, r < count_r - 1
    has_next, has_prev = t < count_t - 1, t > 0
    plan = [
        (1, 0, t, r - 1, has_up, has_down),
        (2, 1, t, r + 1, has_down, has_up),
        (3, 2, t + 1, r, has_next, has_prev),
        (4, 3, t + 1, r - 1, has_next & has_up, has_prev & has_down),
        (5, 4, t + 1, r + 1, has_next & has_down, has_prev & has_up),
    ]
    halo = [
        pltpu.make_async_remote_copy(
            src_ref=snd.at[s], dst_ref=rcv.at[d], send_sem=hs_sem.at[d], recv_sem=hr_sem.at[d],
            device_id=(dt, dr), device_id_type=MESH,
        )
        for s, d, dt, dr, _, _ in plan
    ]
    for copy, (_, _, _, _, sends, _) in zip(halo, plan):
        pl.when(sends)(copy.start)
    tot[...] = snd[0] + bias8[0:1, :]
    for copy, (_, d, _, _, _, gets) in zip(halo, plan):
        def take(copy=copy, d=d):
            copy.wait_recv()
            tot[...] += rcv[d]
        pl.when(gets)(take)
    lat_all[own] = tot[...].astype(BF16)

    side = lax.rem(t, 2)
    mate = t + 1 - 2 * side
    group = count // 2
    place = (t // 2) * count_r + r

    def device(p):
        return (p // count_r) * 2 + side, lax.rem(p, count_r)

    def spread(i):
        dt, dr = device(lax.rem(place + i, group))
        return pltpu.make_async_remote_copy(
            src_ref=lat_all.at[own], dst_ref=lat_all.at[own], send_sem=as_sem.at[i], recv_sem=ar_sem.at[own],
            device_id=(dt, dr), device_id_type=MESH,
        )

    def pass_on(i):
        ft, fr = device(lax.rem(place + group - i, group))
        ident = ft * count_r + fr
        return pltpu.make_async_remote_copy(
            src_ref=lat_all.at[ident], dst_ref=lat_all.at[ident], send_sem=as_sem.at[group + i],
            recv_sem=ar_sem.at[ident], device_id=(mate, r), device_id_type=MESH,
        )

    def from_mate(i):
        ft, fr = device(lax.rem(place + group - i, group))
        ident = (ft + 1 - 2 * side) * count_r + fr
        return pltpu.make_async_remote_copy(
            src_ref=lat_all.at[ident], dst_ref=lat_all.at[ident], send_sem=as_sem.at[group + i],
            recv_sem=ar_sem.at[ident], device_id=(mate, r), device_id_type=MESH,
        )

    def send(i, c):
        spread(i).start()
        return c

    lax.fori_loop(1, group, send, 0)
    pass_on(0).start()
    for c in later:
        c.wait()

    def relay(i, c):
        copy = pass_on(i)
        copy.wait_recv()
        copy.start()
        return c

    lax.fori_loop(1, group, relay, 0)

    def arrive(i, c):
        from_mate(i).wait_recv()
        return c

    lax.fori_loop(0, group, arrive, 0)

    step = 512
    plane = lax.broadcasted_iota(jnp.int32, (half, span), 1)

    def lanes_sum(v):
        out = v[:, 0:128]
        for i in range(1, v.shape[1] // 128):
            out = out + v[:, i * 128 : (i + 1) * 128]
        return out

    def block(j, carry):
        p32 = lat_all[packing[r * count_t + j]].astype(F32)
        left = jnp.concatenate(
            [jnp.where(plane < feats, p32, 0.0), jnp.where(plane < feats, 0.0, p32)], axis=0
        ).astype(BF16)
        total = jnp.zeros((per_block, 128), F32)
        for c in range(0, width, step):
            e = dot(left, pw[:, c : c + step]) + pb[pl.ds(c, step)].reshape(1, step)
            emb[:, c : c + step] = e
            total = total + lanes_sum(e)
        center = jnp.sum(total, axis=1, keepdims=True) / width
        total = jnp.zeros((per_block, 128), F32)
        for c in range(0, width, step):
            d = emb[:, c : c + step] - center
            total = total + lanes_sum(d * d)
        inv = lax.rsqrt(jnp.sum(total, axis=1, keepdims=True) / width + epsilon)
        at = pl.ds(pl.multiple_of(j * per_block, per_block), per_block)
        for c in range(0, width, step):
            gains = 1.0 + scale[pl.ds(c, step)].reshape(1, step)
            moved = shift[pl.ds(c, step)].reshape(1, step)
            mod[at, c : c + step] = ((emb[:, c : c + step] - center) * inv * gains + moved).astype(BF16)
        return carry

    lax.fori_loop(0, count_t, block, 0)

    part = qf.shape[1]
    tile = 256 if part % 256 == 0 else 128

    def out_copy(i, n, src, dst):
        at = pl.ds(pl.multiple_of(n * tile, tile), tile)
        return pltpu.make_async_copy(src.at[:, at], dst.at[:, at], osem.at[i, n])

    heads = ((wq_copy, wq, qb, qf, q_out), (wk_copy, wk, kb, kf, k_out))
    for i, (copy, w, bias, src, dst) in enumerate(heads):
        copy.wait()
        lanes = pl.ds(i * 128, 128)
        sq[:, lanes] = jnp.zeros((tokens, 128), F32)

        def project(n, carry, i=i, w=w, bias=bias, src=src, dst=dst, lanes=lanes):
            at = pl.ds(pl.multiple_of(n * tile, tile), tile)
            v = dot(mod[...], w[:, at]) + bias[at].reshape(1, tile)
            src[:, at] = v
            sq[:, lanes] += lanes_sum(v * v)
            out_copy(i, n, src, dst).start()
            return carry

        lax.fori_loop(0, part // tile, project, 0)

    pick = lax.broadcasted_iota(jnp.int32, (8, 256), 0) // 4 == lax.broadcasted_iota(jnp.int32, (8, 256), 1) // 128
    nt = (((1,), (1,)), ((), ()))
    sums_s[...] = lax.dot_general(
        jnp.where(pick, 1.0, 0.0), sq[...], nt, precision=HIGH, preferred_element_type=F32
    )
    shares = [
        pltpu.make_async_remote_copy(
            src_ref=sums_s, dst_ref=sums_r.at[i - 1], send_sem=ss_sem.at[i - 1], recv_sem=sr_sem.at[i - 1],
            device_id=(lax.rem(t + i, count_t), r), device_id_type=MESH,
        )
        for i in range(1, count_t)
    ]
    for c in shares:
        c.start()
    sums = sums_s[...]
    for i, c in enumerate(shares):
        c.wait_recv()
        sums = sums + sums_r[i]
    inv = lax.rsqrt(sums / width + epsilon)
    first = lax.broadcasted_iota(jnp.int32, (8, 128), 0)
    lane8 = lax.broadcasted_iota(jnp.int32, (8, 128), 1)
    chosen = jnp.where(first == 4 * (lane8 // 64), 1.0, 0.0)
    inv_out[...] = lax.dot_general(inv, chosen, tn, precision=HIGH, preferred_element_type=F32)
    for i, (_, _, _, src, dst) in enumerate(heads):
        for n in range(part // tile):
            out_copy(i, n, src, dst).wait()

    for copy, (_, _, _, _, sends, _) in zip(halo, plan):
        pl.when(sends)(copy.wait_send)

    def sent(i, c):
        spread(i).wait_send()
        return c

    lax.fori_loop(1, group, sent, 0)

    def passed(i, c):
        pass_on(i).wait_send()
        return c

    lax.fori_loop(0, group, passed, 0)
    for c in shares:
        c.wait_send()


def per_device(
    features, block_gain, conv_weight, conv_bias, latent_weight, latent_bias, patch_weight, patch_bias,
    shift_mod, scale_mod, query_weight, query_bias, query_gain, key_weight, key_bias, key_gain, packing,
):
    count_t, count_r = lax.axis_size("tm"), lax.axis_size("rows")
    count = count_t * count_r
    _, _, cols, chans = features.shape
    feats, width = patch_weight.shape
    part = query_weight.shape[1]
    half = cols // 2
    span = 2 * feats
    tokens = count_t * cols
    V = pltpu.VMEM
    operands = (
        packing, features, block_gain, conv_weight, conv_bias, latent_weight.T, latent_bias, patch_weight, patch_bias,
        shift_mod, scale_mod, query_weight, query_bias, key_weight, key_bias,
    )
    like = lambda a: V(a.shape, a.dtype)
    scratch = [like(a) for a in operands[1:7]]
    scratch += [V((2 * feats, width), BF16), like(patch_bias), like(shift_mod), like(scale_mod)]
    scratch += [like(a) for a in operands[11:]]
    scratch += [
        V((3 * chans, 2 * span), BF16),
        V((4 * chans, 6 * span), BF16),
        V((4 * cols, 4 * chans), BF16),
        V((4 * cols, 6 * span), F32),
        V((6, cols, span), F32),
        V((6, half, span), F32),
        V((5, half, span), F32),
        V((half, span), F32),
        V((count, half, span), BF16),
        V((cols, width), F32),
        V((tokens, width), BF16),
        V((tokens, part), F32),
        V((tokens, part), F32),
        V((tokens, 256), F32),
        V((8, tokens), F32),
        V((count_t - 1, 8, tokens), F32),
    ]
    dma = pltpu.SemaphoreType.DMA
    scratch += [dma((12,)), dma((5,)), dma((5,)), dma((5,)), dma((count,)), dma((count,)), dma((count_t - 1,)), dma((count_t - 1,)), dma((2, part // 128))]
    out = jax.ShapeDtypeStruct((tokens, part), F32)
    query, key, inv = pl.pallas_call(
        functools.partial(kernel, count_t, count_r),
        out_shape=(out, out, jax.ShapeDtypeStruct((tokens, 128), F32)),
        in_specs=[pl.BlockSpec(memory_space=pltpu.SMEM)] + [pl.BlockSpec(memory_space=pl.ANY)] * 14,
        out_specs=(pl.BlockSpec(memory_space=pl.ANY),) * 2 + (pl.BlockSpec(memory_space=V),),
        scratch_shapes=scratch,
        compiler_params=pltpu.CompilerParams(collective_id=0, has_side_effects=True, vmem_limit_bytes=67043328),
    )(*operands)
    queries = (query * inv[:, 0:1] * query_gain).astype(BF16)
    keys = (key * inv[:, 64:65] * key_gain).astype(BF16)
    return queries, keys


def solution(mesh):
    in_specs = (
        P("tm", "rows", None, None), P(), P(), P(), P(), P(), P(), P(), P(), P(),
        P(None, "tm"), P("tm"), P("tm"), P(None, "tm"), P("tm"), P("tm"), P(),
    )
    out_specs = (P("rows", "tm"), P("rows", "tm"))
    return jax.shard_map(per_device, mesh=mesh, in_specs=in_specs, out_specs=out_specs, check_vma=False)
```

```python
import functools

import jax
import jax.numpy as jnp
from jax import lax
from jax.experimental import pallas as pl
from jax.experimental.pallas import tpu as pltpu
from jax.sharding import PartitionSpec as P

epsilon = 1e-06
MESH = pl.DeviceIdType.MESH
F32, BF16 = jnp.float32, jnp.bfloat16
HIGH = lax.Precision.HIGHEST


def dot(a, b, **kw):
    return jnp.dot(a, b, preferred_element_type=F32, **kw)


def kernel(
    count_t, count_r,
    packing, feat_h, gain_h, conv_h, cbias_h, lw_h, lbias_h, pw_h, pb_h, shift_h, scale_h,
    wq_h, qb_h, wk_h, kb_h,
    q_out, k_out, inv_out,
    feat, gain, conv, cbias, lw, lbias, pw, pb, shift, scale, wq, qb, wk, kb,
    rb, km, lhs, y_ref, fold, snd, rcv, tot, lat_all, emb, mod, tiles, sq, sums_s, sums_r,
    lsem, wsem, hs_sem, hr_sem, as_sem, ar_sem, ss_sem, sr_sem, osem,
):
    t, r = lax.axis_index("tm"), lax.axis_index("rows")
    count = count_t * count_r
    own = t * count_r + r
    _, _, cols, chans = feat.shape
    width = emb.shape[1]
    half = cols // 2
    feats = pw_h.shape[0]
    tokens = mod.shape[0]
    per_block = 2 * half

    small = [(feat_h, feat), (gain_h, gain), (lw_h, lw), (cbias_h, cbias), (lbias_h, lbias)]
    late = [
        (pw_h, pw.at[pl.ds(0, feats)]), (pw_h, pw.at[pl.ds(feats, feats)]), (pb_h, pb), (shift_h, shift),
        (scale_h, scale), (qb_h, qb), (kb_h, kb),
    ]
    copies = [pltpu.make_async_copy(s, d, lsem.at[i]) for i, (s, d) in enumerate(small + late)]
    early, later = copies[: len(small)], copies[len(small) :]
    for c in early:
        c.start()
    conv_copies = [pltpu.make_async_copy(conv_h.at[:, b], conv.at[:, b], wsem.at[b]) for b in range(3)]
    for c in conv_copies:
        c.start()
    for c in later:
        c.start()
    wq_copy = pltpu.make_async_copy(wq_h, wq, wsem.at[3])
    wk_copy = pltpu.make_async_copy(wk_h, wk, wsem.at[4])

    barrier = pltpu.get_barrier_semaphore()

    def greet(i, c):
        other = lax.rem(own + i, count)
        pl.semaphore_signal(barrier, inc=1, device_id=(other // count_r, lax.rem(other, count_r)), device_id_type=MESH)
        return c

    lax.fori_loop(1, count, greet, 0)

    for c in early:
        c.wait()

    lats = lw.shape[0]
    tn = (((0,), (0,)), ((), ()))
    li = lax.broadcasted_iota(jnp.int32, (lats, 2 * feats), 0)
    lj = lax.broadcasted_iota(jnp.int32, (lats, 2 * feats), 1)
    both = ((lj % feats) // 4) == li
    e_both = jnp.where(both, 1.0, 0.0)
    e_low = jnp.where(both & (lj < feats), 1.0, 0.0)
    e_high = jnp.where(both & (lj >= feats), 1.0, 0.0)
    lwv = lw[...]
    lw_low = lax.dot_general(lwv, e_low.astype(BF16), tn, preferred_element_type=F32).astype(BF16)
    lw_high = lax.dot_general(lwv, e_high.astype(BF16), tn, preferred_element_type=F32).astype(BF16)
    lw_both = lax.dot_general(lwv, e_both.astype(BF16), tn, preferred_element_type=F32).astype(BF16)
    span = 2 * feats
    rb[...] = jnp.zeros(rb.shape, BF16)
    rb[pl.ds(0, chans), pl.ds(0, span)] = lw_low
    rb[pl.ds(chans, chans), pl.ds(0, span)] = lw_high
    rb[pl.ds(2 * chans, chans), pl.ds(span, span)] = lw_both
    km[pl.ds(3 * chans, chans), :] = jnp.zeros((chans, km.shape[1]), BF16)
    km[pl.ds(3 * chans, chans), pl.ds(2 * span, span)] = lw_low
    cb8 = jnp.broadcast_to(cbias[...].reshape(1, chans), (8, chans))
    lb8 = jnp.broadcast_to(lbias[...].reshape(1, lats), (8, lats))
    bias8 = dot(cb8, lw_both.astype(F32), precision=HIGH) + dot(lb8, e_both, precision=HIGH)

    gain_v = gain[...].reshape(1, chans)
    row_at = lax.broadcasted_iota(jnp.int32, (cols, chans), 0)
    for f in range(2):
        for w in range(2):
            raw = feat[f, w]
            v = raw.astype(F32)
            sm = jnp.mean(v * v, axis=-1, keepdims=True)
            x = v * lax.rsqrt(sm + epsilon) * gain_v
            act = (x / (1.0 + jnp.exp(-x))).astype(BF16)
            a32 = act.astype(F32)
            prev = jnp.where(row_at == 0, 0.0, pltpu.roll(a32, 1, 0))
            nxt = jnp.where(row_at == cols - 1, 0.0, pltpu.roll(a32, cols - 1, 0))
            at = pl.ds((f * 2 + w) * cols, cols)
            lhs[at, pl.ds(0, chans)] = prev.astype(BF16)
            lhs[at, pl.ds(chans, chans)] = act
            lhs[at, pl.ds(2 * chans, chans)] = nxt.astype(BF16)
            lhs[at, pl.ds(3 * chans, chans)] = raw

    rbv = rb[...]
    for b in range(3):
        conv_copies[b].wait()
        if b == 2:
            wq_copy.start()
            wk_copy.start()
        for e in range(3):
            w3 = jnp.concatenate([conv[2, b, e], conv[1, b, e], conv[0, b, e]], axis=1)
            km[pl.ds(e * chans, chans), pl.ds(b * 2 * span, 2 * span)] = dot(w3, rbv).astype(BF16)
        at = pl.ds(b * 2 * span, 2 * span)
        y_ref[:, at] = dot(lhs[...], km[:, at])

    lane = lax.broadcasted_iota(jnp.int32, (cols, span), 1)
    row = lax.broadcasted_iota(jnp.int32, (cols, span), 0)
    even_row = (lane & 2) == 0
    low = lane < feats
    parity = (lane & 1) == (row & 1)

    def y(f, w, b, z):
        return y_ref[pl.ds((f * 2 + w) * cols, cols), pl.ds(b * 2 * span + z * span, span)]

    def mid(f, z):
        return jnp.where(even_row, y(f, 0, 1, z) + y(f, 1, 2, z), y(f, 0, 0, z) + y(f, 1, 1, z))

    def up(f, z):
        return jnp.where(even_row, 0.0, y(f, 0, 2, z))

    def down(f, z):
        return jnp.where(even_row, y(f, 1, 0, z), 0.0)

    for i, part in enumerate((mid, up, down)):
        x0, x1 = part(0, 0), pltpu.roll(part(1, 0), feats, 1)
        mine = jnp.where(low, x0, x0 + x1)
        after = jnp.where(low, x1 + part(0, 1), part(1, 1))
        fold[i] = jnp.where(parity, mine, 0.0)
        fold[3 + i] = jnp.where(parity, after, 0.0)
    for i in range(6):
        snd[i] = fold[i, pl.ds(0, half, 2), :] + fold[i, pl.ds(1, half, 2), :]

    pl.semaphore_wait(barrier, count - 1)

    has_up, has_down = r > 0, r < count_r - 1
    has_next, has_prev = t < count_t - 1, t > 0
    plan = [
        (1, 0, t, r - 1, has_up, has_down),
        (2, 1, t, r + 1, has_down, has_up),
        (3, 2, t + 1, r, has_next, has_prev),
        (4, 3, t + 1, r - 1, has_next & has_up, has_prev & has_down),
        (5, 4, t + 1, r + 1, has_next & has_down, has_prev & has_up),
    ]
    halo = [
        pltpu.make_async_remote_copy(
            src_ref=snd.at[s], dst_ref=rcv.at[d], send_sem=hs_sem.at[d], recv_sem=hr_sem.at[d],
            device_id=(dt, dr), device_id_type=MESH,
        )
        for s, d, dt, dr, _, _ in plan
    ]
    for copy, (_, _, _, _, sends, _) in zip(halo, plan):
        pl.when(sends)(copy.start)
    tot[...] = snd[0] + bias8[0:1, :]
    for copy, (_, d, _, _, _, gets) in zip(halo, plan):
        def take(copy=copy, d=d):
            copy.wait_recv()
            tot[...] += rcv[d]
        pl.when(gets)(take)
    lat_all[own] = tot[...].astype(BF16)

    side = lax.rem(t, 2)
    mate = t + 1 - 2 * side
    group = count // 2
    place = (t // 2) * count_r + r

    def device(p):
        return (p // count_r) * 2 + side, lax.rem(p, count_r)

    def spread(i):
        dt, dr = device(lax.rem(place + i, group))
        return pltpu.make_async_remote_copy(
            src_ref=lat_all.at[own], dst_ref=lat_all.at[own], send_sem=as_sem.at[i], recv_sem=ar_sem.at[own],
            device_id=(dt, dr), device_id_type=MESH,
        )

    def pass_on(i):
        ft, fr = device(lax.rem(place + group - i, group))
        ident = ft * count_r + fr
        return pltpu.make_async_remote_copy(
            src_ref=lat_all.at[ident], dst_ref=lat_all.at[ident], send_sem=as_sem.at[group + i],
            recv_sem=ar_sem.at[ident], device_id=(mate, r), device_id_type=MESH,
        )

    def from_mate(i):
        ft, fr = device(lax.rem(place + group - i, group))
        ident = (ft + 1 - 2 * side) * count_r + fr
        return pltpu.make_async_remote_copy(
            src_ref=lat_all.at[ident], dst_ref=lat_all.at[ident], send_sem=as_sem.at[group + i],
            recv_sem=ar_sem.at[ident], device_id=(mate, r), device_id_type=MESH,
        )

    def send(i, c):
        spread(i).start()
        return c

    lax.fori_loop(1, group, send, 0)
    pass_on(0).start()
    for c in later:
        c.wait()

    def relay(i, c):
        copy = pass_on(i)
        copy.wait_recv()
        copy.start()
        return c

    lax.fori_loop(1, group, relay, 0)

    def arrive(i, c):
        from_mate(i).wait_recv()
        return c

    lax.fori_loop(0, group, arrive, 0)

    step = 512
    plane = lax.broadcasted_iota(jnp.int32, (half, span), 1)

    def lanes_sum(v):
        out = v[:, 0:128]
        for i in range(1, v.shape[1] // 128):
            out = out + v[:, i * 128 : (i + 1) * 128]
        return out

    def block(j, carry):
        p32 = lat_all[packing[r * count_t + j]].astype(F32)
        left = jnp.concatenate(
            [jnp.where(plane < feats, p32, 0.0), jnp.where(plane < feats, 0.0, p32)], axis=0
        ).astype(BF16)
        total = jnp.zeros((per_block, 128), F32)
        for c in range(0, width, step):
            e = dot(left, pw[:, c : c + step]) + pb[pl.ds(c, step)].reshape(1, step)
            emb[:, c : c + step] = e
            total = total + lanes_sum(e)
        center = jnp.sum(total, axis=1, keepdims=True) / width
        total = jnp.zeros((per_block, 128), F32)
        for c in range(0, width, step):
            d = emb[:, c : c + step] - center
            total = total + lanes_sum(d * d)
        inv = lax.rsqrt(jnp.sum(total, axis=1, keepdims=True) / width + epsilon)
        at = pl.ds(pl.multiple_of(j * per_block, per_block), per_block)
        for c in range(0, width, step):
            gains = 1.0 + scale[pl.ds(c, step)].reshape(1, step)
            moved = shift[pl.ds(c, step)].reshape(1, step)
            mod[at, c : c + step] = ((emb[:, c : c + step] - center) * inv * gains + moved).astype(BF16)
        return carry

    lax.fori_loop(0, count_t, block, 0)

    part = wq.shape[1]
    tile = tiles.shape[2]
    count_n = part // tile

    def out_copy(i, n, dst):
        at = pl.ds(pl.multiple_of(n * tile, tile), tile)
        return pltpu.make_async_copy(tiles.at[lax.rem(i * count_n + n, 2)], dst.at[:, at], osem.at[i, n])

    heads = ((wq_copy, wq, qb, q_out), (wk_copy, wk, kb, k_out))
    for i, (copy, w, bias, dst) in enumerate(heads):
        copy.wait()
        lanes = pl.ds(i * 128, 128)
        sq[:, lanes] = jnp.zeros((tokens, 128), F32)

        def project(n, carry, i=i, w=w, bias=bias, dst=dst, lanes=lanes):
            at = pl.ds(pl.multiple_of(n * tile, tile), tile)
            pl.when(n >= 2)(lambda: out_copy(i, n - 2, dst).wait())
            if i:
                pl.when(n < 2)(lambda: out_copy(0, count_n - 2 + n, heads[0][3]).wait())
            v = dot(mod[...], w[:, at]) + bias[at].reshape(1, tile)
            tiles[lax.rem(i * count_n + n, 2)] = v
            sq[:, lanes] += lanes_sum(v * v)
            out_copy(i, n, dst).start()
            return carry

        lax.fori_loop(0, count_n, project, 0)

    pick = lax.broadcasted_iota(jnp.int32, (8, 256), 0) // 4 == lax.broadcasted_iota(jnp.int32, (8, 256), 1) // 128
    nt = (((1,), (1,)), ((), ()))
    sums_s[...] = lax.dot_general(
        jnp.where(pick, 1.0, 0.0), sq[...], nt, precision=HIGH, preferred_element_type=F32
    )
    shares = [
        pltpu.make_async_remote_copy(
            src_ref=sums_s, dst_ref=sums_r.at[i - 1], send_sem=ss_sem.at[i - 1], recv_sem=sr_sem.at[i - 1],
            device_id=(lax.rem(t + i, count_t), r), device_id_type=MESH,
        )
        for i in range(1, count_t)
    ]
    for c in shares:
        c.start()
    sums = sums_s[...]
    for i, c in enumerate(shares):
        c.wait_recv()
        sums = sums + sums_r[i]
    inv = lax.rsqrt(sums / width + epsilon)
    first = lax.broadcasted_iota(jnp.int32, (8, 256), 0)
    lane8 = lax.broadcasted_iota(jnp.int32, (8, 256), 1)
    chosen = jnp.where(first == 4 * (lane8 // 128), 1.0, 0.0)
    inv_out[...] = lax.dot_general(inv, chosen, tn, precision=HIGH, preferred_element_type=F32)
    for n in range(count_n - 2, count_n):
        out_copy(1, n, k_out).wait()

    for copy, (_, _, _, _, sends, _) in zip(halo, plan):
        pl.when(sends)(copy.wait_send)

    def sent(i, c):
        spread(i).wait_send()
        return c

    lax.fori_loop(1, group, sent, 0)

    def passed(i, c):
        pass_on(i).wait_send()
        return c

    lax.fori_loop(0, group, passed, 0)
    for c in shares:
        c.wait_send()


def per_device(
    features, block_gain, conv_weight, conv_bias, latent_weight, latent_bias, patch_weight, patch_bias,
    shift_mod, scale_mod, query_weight, query_bias, query_gain, key_weight, key_bias, key_gain, packing,
):
    count_t, count_r = lax.axis_size("tm"), lax.axis_size("rows")
    count = count_t * count_r
    _, _, cols, chans = features.shape
    feats, width = patch_weight.shape
    part = query_weight.shape[1]
    half = cols // 2
    span = 2 * feats
    tokens = count_t * cols
    tile = 256 if part % 256 == 0 else 128
    V = pltpu.VMEM
    operands = (
        packing, features, block_gain, conv_weight, conv_bias, latent_weight.T, latent_bias, patch_weight, patch_bias,
        shift_mod, scale_mod, query_weight, query_bias, key_weight, key_bias,
    )
    like = lambda a: V(a.shape, a.dtype)
    scratch = [like(a) for a in operands[1:7]]
    scratch += [V((2 * feats, width), BF16), like(patch_bias), like(shift_mod), like(scale_mod)]
    scratch += [like(a) for a in operands[11:]]
    scratch += [
        V((3 * chans, 2 * span), BF16),
        V((4 * chans, 6 * span), BF16),
        V((4 * cols, 4 * chans), BF16),
        V((4 * cols, 6 * span), F32),
        V((6, cols, span), F32),
        V((6, half, span), F32),
        V((5, half, span), F32),
        V((half, span), F32),
        V((count, half, span), BF16),
        V((cols, width), F32),
        V((tokens, width), BF16),
        V((2, tokens, tile), F32),
        V((tokens, 256), F32),
        V((8, tokens), F32),
        V((count_t - 1, 8, tokens), F32),
    ]
    dma = pltpu.SemaphoreType.DMA
    scratch += [dma((12,)), dma((5,)), dma((5,)), dma((5,)), dma((count,)), dma((count,)), dma((count_t - 1,)), dma((count_t - 1,)), dma((2, part // 128))]
    out = jax.ShapeDtypeStruct((tokens, part), F32)
    query, key, inv = pl.pallas_call(
        functools.partial(kernel, count_t, count_r),
        out_shape=(out, out, jax.ShapeDtypeStruct((tokens, 256), F32)),
        in_specs=[pl.BlockSpec(memory_space=pltpu.SMEM)] + [pl.BlockSpec(memory_space=pl.ANY)] * 14,
        out_specs=(pl.BlockSpec(memory_space=pl.ANY),) * 2 + (pl.BlockSpec(memory_space=V),),
        scratch_shapes=scratch,
        compiler_params=pltpu.CompilerParams(collective_id=0, has_side_effects=True, vmem_limit_bytes=67043328),
    )(*operands)
    return finish(query, key, inv, query_gain, key_gain)


def scaled(q_h, k_h, inv, qg, kg, qo_h, ko_h, q, k, qo, ko, in_sem, out_sem):
    chunks, _, part = q.shape[0], q.shape[1], q.shape[2]
    rows = q.shape[1]
    both = ((q_h, q, qg, qo, qo_h), (k_h, k, kg, ko, ko_h))
    loads, stores = [], []
    for c in range(chunks):
        for i, (src, buf, _, obuf, dst) in enumerate(both):
            at = pl.ds(c * rows, rows)
            loads.append(pltpu.make_async_copy(src.at[at], buf.at[c], in_sem.at[i, c]))
            stores.append(pltpu.make_async_copy(obuf.at[c], dst.at[at], out_sem.at[i, c]))
    for copy in loads:
        copy.start()
    for c in range(chunks):
        for i, (_, buf, gain, obuf, _) in enumerate(both):
            loads[2 * c + i].wait()
            factor = inv[pl.ds(c * rows, rows), pl.ds(i * 128, 128)]
            for n in range(0, part, 128):
                at = pl.ds(n, 128)
                obuf[c, :, at] = (buf[c, :, at] * factor * gain[at].reshape(1, 128)).astype(BF16)
            stores[2 * c + i].start()
    for copy in stores:
        copy.wait()


def finish(query, key, inv, query_gain, key_gain):
    tokens, part = query.shape
    chunks = tokens // 128
    out = jax.ShapeDtypeStruct((tokens, part), BF16)
    V, dma = pltpu.VMEM, pltpu.SemaphoreType.DMA
    return pl.pallas_call(
        scaled,
        out_shape=(out, out),
        in_specs=[pl.BlockSpec(memory_space=pl.ANY)] * 2 + [pl.BlockSpec(memory_space=V)] * 3,
        out_specs=(pl.BlockSpec(memory_space=pl.ANY),) * 2,
        scratch_shapes=[
            V((chunks, 128, part), F32), V((chunks, 128, part), F32), V((chunks, 128, part), BF16), V((chunks, 128, part), BF16),
            dma((2, chunks)), dma((2, chunks)),
        ],
        compiler_params=pltpu.CompilerParams(vmem_limit_bytes=67043328),
    )(query, key, inv, query_gain, key_gain)


def solution(mesh):
    in_specs = (
        P("tm", "rows", None, None), P(), P(), P(), P(), P(), P(), P(), P(), P(),
        P(None, "tm"), P("tm"), P("tm"), P(None, "tm"), P("tm"), P("tm"), P(),
    )
    out_specs = (P("rows", "tm"), P("rows", "tm"))
    return jax.shard_map(per_device, mesh=mesh, in_specs=in_specs, out_specs=out_specs, check_vma=False)
```

```python
import functools

import jax
import jax.numpy as jnp
from jax import lax
from jax.experimental import pallas as pl
from jax.experimental.pallas import tpu as pltpu
from jax.sharding import PartitionSpec as P

epsilon = 1e-06
MESH = pl.DeviceIdType.MESH
F32, BF16 = jnp.float32, jnp.bfloat16
HIGH = lax.Precision.HIGHEST


def dot(a, b, **kw):
    return jnp.dot(a, b, preferred_element_type=F32, **kw)


def kernel(
    count_t, count_r,
    packing, feat_h, gain_h, conv_h, cbias_h, lw_h, lbias_h, pw_h, pb_h, shift_h, scale_h,
    wq_h, qb_h, wk_h, kb_h,
    q_out, k_out, inv_out,
    feat, gain, conv, cbias, lw, lbias, pw, pb, shift, scale, wq, qb, wk, kb,
    rb, km, lhs, y_ref, fold, snd, rcv, tot, lat_all, emb, mod, tiles, sq, sums_s, sums_r,
    lsem, wsem, hs_sem, hr_sem, as_sem, ar_sem, ss_sem, sr_sem, osem,
):
    t, r = lax.axis_index("tm"), lax.axis_index("rows")
    count = count_t * count_r
    own = t * count_r + r
    _, _, cols, chans = feat.shape
    width = emb.shape[1]
    half = cols // 2
    feats = pw_h.shape[0]
    tokens = mod.shape[0]
    per_block = 2 * half

    small = [(feat_h, feat), (gain_h, gain), (lw_h, lw), (cbias_h, cbias), (lbias_h, lbias)]
    late = [
        (pw_h, pw.at[pl.ds(0, feats)]), (pw_h, pw.at[pl.ds(feats, feats)]), (pb_h, pb), (shift_h, shift),
        (scale_h, scale), (qb_h, qb), (kb_h, kb),
    ]
    copies = [pltpu.make_async_copy(s, d, lsem.at[i]) for i, (s, d) in enumerate(small + late)]
    early, later = copies[: len(small)], copies[len(small) :]
    for c in early:
        c.start()
    conv_copies = [pltpu.make_async_copy(conv_h.at[:, b], conv.at[:, b], wsem.at[b]) for b in range(3)]
    for c in conv_copies:
        c.start()
    for c in later:
        c.start()
    wq_copy = pltpu.make_async_copy(wq_h, wq, wsem.at[3])
    wk_copy = pltpu.make_async_copy(wk_h, wk, wsem.at[4])

    barrier = pltpu.get_barrier_semaphore()

    def greet(i, c):
        other = lax.rem(own + i, count)
        pl.semaphore_signal(barrier, inc=1, device_id=(other // count_r, lax.rem(other, count_r)), device_id_type=MESH)
        return c

    lax.fori_loop(1, count, greet, 0)

    for c in early:
        c.wait()

    lats = lw.shape[0]
    tn = (((0,), (0,)), ((), ()))
    li = lax.broadcasted_iota(jnp.int32, (lats, 2 * feats), 0)
    lj = lax.broadcasted_iota(jnp.int32, (lats, 2 * feats), 1)
    both = ((lj % feats) // 4) == li
    e_both = jnp.where(both, 1.0, 0.0)
    e_low = jnp.where(both & (lj < feats), 1.0, 0.0)
    e_high = jnp.where(both & (lj >= feats), 1.0, 0.0)
    lwv = lw[...]
    lw_low = lax.dot_general(lwv, e_low.astype(BF16), tn, preferred_element_type=F32).astype(BF16)
    lw_high = lax.dot_general(lwv, e_high.astype(BF16), tn, preferred_element_type=F32).astype(BF16)
    lw_both = lax.dot_general(lwv, e_both.astype(BF16), tn, preferred_element_type=F32).astype(BF16)
    span = 2 * feats
    rb[...] = jnp.zeros(rb.shape, BF16)
    rb[pl.ds(0, chans), pl.ds(0, span)] = lw_low
    rb[pl.ds(chans, chans), pl.ds(0, span)] = lw_high
    rb[pl.ds(2 * chans, chans), pl.ds(span, span)] = lw_both
    km[pl.ds(3 * chans, chans), :] = jnp.zeros((chans, km.shape[1]), BF16)
    km[pl.ds(3 * chans, chans), pl.ds(2 * span, span)] = lw_low
    cb8 = jnp.broadcast_to(cbias[...].reshape(1, chans), (8, chans))
    lb8 = jnp.broadcast_to(lbias[...].reshape(1, lats), (8, lats))
    bias8 = dot(cb8, lw_both.astype(F32), precision=HIGH) + dot(lb8, e_both, precision=HIGH)

    gain_v = gain[...].reshape(1, chans)
    row_at = lax.broadcasted_iota(jnp.int32, (cols, chans), 0)
    for f in range(2):
        for w in range(2):
            raw = feat[f, w]
            v = raw.astype(F32)
            sm = jnp.mean(v * v, axis=-1, keepdims=True)
            x = v * lax.rsqrt(sm + epsilon) * gain_v
            act = (x / (1.0 + jnp.exp(-x))).astype(BF16)
            a32 = act.astype(F32)
            prev = jnp.where(row_at == 0, 0.0, pltpu.roll(a32, 1, 0))
            nxt = jnp.where(row_at == cols - 1, 0.0, pltpu.roll(a32, cols - 1, 0))
            at = pl.ds((f * 2 + w) * cols, cols)
            lhs[at, pl.ds(0, chans)] = prev.astype(BF16)
            lhs[at, pl.ds(chans, chans)] = act
            lhs[at, pl.ds(2 * chans, chans)] = nxt.astype(BF16)
            lhs[at, pl.ds(3 * chans, chans)] = raw

    rbv = rb[...]
    for b in range(3):
        conv_copies[b].wait()
        if b == 2:
            wq_copy.start()
            wk_copy.start()
        for e in range(3):
            w3 = jnp.concatenate([conv[2, b, e], conv[1, b, e], conv[0, b, e]], axis=1)
            km[pl.ds(e * chans, chans), pl.ds(b * 2 * span, 2 * span)] = dot(w3, rbv).astype(BF16)
        at = pl.ds(b * 2 * span, 2 * span)
        y_ref[:, at] = dot(lhs[...], km[:, at])

    lane = lax.broadcasted_iota(jnp.int32, (cols, span), 1)
    row = lax.broadcasted_iota(jnp.int32, (cols, span), 0)
    even_row = (lane & 2) == 0
    low = lane < feats
    parity = (lane & 1) == (row & 1)

    def y(f, w, b, z):
        return y_ref[pl.ds((f * 2 + w) * cols, cols), pl.ds(b * 2 * span + z * span, span)]

    def mid(f, z):
        return jnp.where(even_row, y(f, 0, 1, z) + y(f, 1, 2, z), y(f, 0, 0, z) + y(f, 1, 1, z))

    def up(f, z):
        return jnp.where(even_row, 0.0, y(f, 0, 2, z))

    def down(f, z):
        return jnp.where(even_row, y(f, 1, 0, z), 0.0)

    for i, part in enumerate((mid, up, down)):
        x0, x1 = part(0, 0), pltpu.roll(part(1, 0), feats, 1)
        mine = jnp.where(low, x0, x0 + x1)
        after = jnp.where(low, x1 + part(0, 1), part(1, 1))
        fold[i] = jnp.where(parity, mine, 0.0)
        fold[3 + i] = jnp.where(parity, after, 0.0)
    for i in range(6):
        snd[i] = fold[i, pl.ds(0, half, 2), :] + fold[i, pl.ds(1, half, 2), :]

    pl.semaphore_wait(barrier, count - 1)

    has_up, has_down = r > 0, r < count_r - 1
    has_next, has_prev = t < count_t - 1, t > 0
    plan = [
        (1, 0, t, r - 1, has_up, has_down),
        (2, 1, t, r + 1, has_down, has_up),
        (3, 2, t + 1, r, has_next, has_prev),
        (4, 3, t + 1, r - 1, has_next & has_up, has_prev & has_down),
        (5, 4, t + 1, r + 1, has_next & has_down, has_prev & has_up),
    ]
    halo = [
        pltpu.make_async_remote_copy(
            src_ref=snd.at[s], dst_ref=rcv.at[d], send_sem=hs_sem.at[d], recv_sem=hr_sem.at[d],
            device_id=(dt, dr), device_id_type=MESH,
        )
        for s, d, dt, dr, _, _ in plan
    ]
    for copy, (_, _, _, _, sends, _) in zip(halo, plan):
        pl.when(sends)(copy.start)
    tot[...] = snd[0] + bias8[0:1, :]
    for copy, (_, d, _, _, _, gets) in zip(halo, plan):
        def take(copy=copy, d=d):
            copy.wait_recv()
            tot[...] += rcv[d]
        pl.when(gets)(take)
    lat_all[own] = tot[...].astype(BF16)

    side = lax.rem(t, 2)
    mate = t + 1 - 2 * side
    group = count // 2
    place = (t // 2) * count_r + r

    def device(p):
        return (p // count_r) * 2 + side, lax.rem(p, count_r)

    def spread(i):
        dt, dr = device(lax.rem(place + i, group))
        return pltpu.make_async_remote_copy(
            src_ref=lat_all.at[own], dst_ref=lat_all.at[own], send_sem=as_sem.at[i], recv_sem=ar_sem.at[own],
            device_id=(dt, dr), device_id_type=MESH,
        )

    def pass_on(i):
        ft, fr = device(lax.rem(place + group - i, group))
        ident = ft * count_r + fr
        return pltpu.make_async_remote_copy(
            src_ref=lat_all.at[ident], dst_ref=lat_all.at[ident], send_sem=as_sem.at[group + i],
            recv_sem=ar_sem.at[ident], device_id=(mate, r), device_id_type=MESH,
        )

    def from_mate(i):
        ft, fr = device(lax.rem(place + group - i, group))
        ident = (ft + 1 - 2 * side) * count_r + fr
        return pltpu.make_async_remote_copy(
            src_ref=lat_all.at[ident], dst_ref=lat_all.at[ident], send_sem=as_sem.at[group + i],
            recv_sem=ar_sem.at[ident], device_id=(mate, r), device_id_type=MESH,
        )

    def send(i, c):
        spread(i).start()
        return c

    lax.fori_loop(1, group, send, 0)
    pass_on(0).start()
    for c in later:
        c.wait()

    def relay(i, c):
        copy = pass_on(i)
        copy.wait_recv()
        copy.start()
        return c

    lax.fori_loop(1, group, relay, 0)

    def arrive(i, c):
        from_mate(i).wait_recv()
        return c

    lax.fori_loop(0, group, arrive, 0)

    step = 512
    plane = lax.broadcasted_iota(jnp.int32, (half, span), 1)

    def lanes_sum(v):
        out = v[:, 0:128]
        for i in range(1, v.shape[1] // 128):
            out = out + v[:, i * 128 : (i + 1) * 128]
        return out

    def block(j, carry):
        p32 = lat_all[packing[r * count_t + j]].astype(F32)
        left = jnp.concatenate(
            [jnp.where(plane < feats, p32, 0.0), jnp.where(plane < feats, 0.0, p32)], axis=0
        ).astype(BF16)
        total = jnp.zeros((per_block, 128), F32)
        for c in range(0, width, step):
            e = dot(left, pw[:, c : c + step]) + pb[pl.ds(c, step)].reshape(1, step)
            emb[:, c : c + step] = e
            total = total + lanes_sum(e)
        center = jnp.sum(total, axis=1, keepdims=True) / width
        total = jnp.zeros((per_block, 128), F32)
        for c in range(0, width, step):
            d = emb[:, c : c + step] - center
            total = total + lanes_sum(d * d)
        inv = lax.rsqrt(jnp.sum(total, axis=1, keepdims=True) / width + epsilon)
        at = pl.ds(pl.multiple_of(j * per_block, per_block), per_block)
        for c in range(0, width, step):
            gains = 1.0 + scale[pl.ds(c, step)].reshape(1, step)
            moved = shift[pl.ds(c, step)].reshape(1, step)
            mod[at, c : c + step] = ((emb[:, c : c + step] - center) * inv * gains + moved).astype(BF16)
        return carry

    lax.fori_loop(0, count_t, block, 0)

    part = wq.shape[1]
    tile = tiles.shape[2]
    count_n = part // tile

    def out_copy(i, n, dst):
        at = pl.ds(pl.multiple_of(n * tile, tile), tile)
        return pltpu.make_async_copy(tiles.at[lax.rem(i * count_n + n, 2)], dst.at[:, at], osem.at[i, n])

    heads = ((wq_copy, wq, qb, q_out), (wk_copy, wk, kb, k_out))
    for i, (copy, w, bias, dst) in enumerate(heads):
        copy.wait()
        lanes = pl.ds(i * 128, 128)
        sq[:, lanes] = jnp.zeros((tokens, 128), F32)

        def project(n, carry, i=i, w=w, bias=bias, dst=dst, lanes=lanes):
            at = pl.ds(pl.multiple_of(n * tile, tile), tile)
            pl.when(n >= 2)(lambda: out_copy(i, n - 2, dst).wait())
            if i:
                pl.when(n < 2)(lambda: out_copy(0, count_n - 2 + n, heads[0][3]).wait())
            v = dot(mod[...], w[:, at]) + bias[at].reshape(1, tile)
            tiles[lax.rem(i * count_n + n, 2)] = v.astype(BF16)
            sq[:, lanes] += lanes_sum(v * v)
            out_copy(i, n, dst).start()
            return carry

        lax.fori_loop(0, count_n, project, 0)

    pick = lax.broadcasted_iota(jnp.int32, (8, 256), 0) // 4 == lax.broadcasted_iota(jnp.int32, (8, 256), 1) // 128
    nt = (((1,), (1,)), ((), ()))
    sums_s[...] = lax.dot_general(
        jnp.where(pick, 1.0, 0.0), sq[...], nt, precision=HIGH, preferred_element_type=F32
    )
    shares = [
        pltpu.make_async_remote_copy(
            src_ref=sums_s, dst_ref=sums_r.at[i - 1], send_sem=ss_sem.at[i - 1], recv_sem=sr_sem.at[i - 1],
            device_id=(lax.rem(t + i, count_t), r), device_id_type=MESH,
        )
        for i in range(1, count_t)
    ]
    for c in shares:
        c.start()
    sums = sums_s[...]
    for i, c in enumerate(shares):
        c.wait_recv()
        sums = sums + sums_r[i]
    inv = lax.rsqrt(sums / width + epsilon)
    first = lax.broadcasted_iota(jnp.int32, (8, 256), 0)
    lane8 = lax.broadcasted_iota(jnp.int32, (8, 256), 1)
    chosen = jnp.where(first == 4 * (lane8 // 128), 1.0, 0.0)
    inv_out[...] = lax.dot_general(inv, chosen, tn, precision=HIGH, preferred_element_type=F32)
    for n in range(count_n - 2, count_n):
        out_copy(1, n, k_out).wait()

    for copy, (_, _, _, _, sends, _) in zip(halo, plan):
        pl.when(sends)(copy.wait_send)

    def sent(i, c):
        spread(i).wait_send()
        return c

    lax.fori_loop(1, group, sent, 0)

    def passed(i, c):
        pass_on(i).wait_send()
        return c

    lax.fori_loop(0, group, passed, 0)
    for c in shares:
        c.wait_send()


def per_device(
    features, block_gain, conv_weight, conv_bias, latent_weight, latent_bias, patch_weight, patch_bias,
    shift_mod, scale_mod, query_weight, query_bias, query_gain, key_weight, key_bias, key_gain, packing,
):
    count_t, count_r = lax.axis_size("tm"), lax.axis_size("rows")
    count = count_t * count_r
    _, _, cols, chans = features.shape
    feats, width = patch_weight.shape
    part = query_weight.shape[1]
    half = cols // 2
    span = 2 * feats
    tokens = count_t * cols
    tile = 256 if part % 256 == 0 else 128
    V = pltpu.VMEM
    operands = (
        packing, features, block_gain, conv_weight, conv_bias, latent_weight.T, latent_bias, patch_weight, patch_bias,
        shift_mod, scale_mod, query_weight, query_bias, key_weight, key_bias,
    )
    like = lambda a: V(a.shape, a.dtype)
    scratch = [like(a) for a in operands[1:7]]
    scratch += [V((2 * feats, width), BF16), like(patch_bias), like(shift_mod), like(scale_mod)]
    scratch += [like(a) for a in operands[11:]]
    scratch += [
        V((3 * chans, 2 * span), BF16),
        V((4 * chans, 6 * span), BF16),
        V((4 * cols, 4 * chans), BF16),
        V((4 * cols, 6 * span), F32),
        V((6, cols, span), F32),
        V((6, half, span), F32),
        V((5, half, span), F32),
        V((half, span), F32),
        V((count, half, span), BF16),
        V((cols, width), F32),
        V((tokens, width), BF16),
        V((2, tokens, tile), BF16),
        V((tokens, 256), F32),
        V((8, tokens), F32),
        V((count_t - 1, 8, tokens), F32),
    ]
    dma = pltpu.SemaphoreType.DMA
    scratch += [dma((12,)), dma((5,)), dma((5,)), dma((5,)), dma((count,)), dma((count,)), dma((count_t - 1,)), dma((count_t - 1,)), dma((2, part // 128))]
    out = jax.ShapeDtypeStruct((tokens, part), BF16)
    query, key, inv = pl.pallas_call(
        functools.partial(kernel, count_t, count_r),
        out_shape=(out, out, jax.ShapeDtypeStruct((tokens, 256), F32)),
        in_specs=[pl.BlockSpec(memory_space=pltpu.SMEM)] + [pl.BlockSpec(memory_space=pl.ANY)] * 14,
        out_specs=(pl.BlockSpec(memory_space=pl.ANY),) * 2 + (pl.BlockSpec(memory_space=V),),
        scratch_shapes=scratch,
        compiler_params=pltpu.CompilerParams(collective_id=0, has_side_effects=True, vmem_limit_bytes=67043328),
    )(*operands)
    return finish(query, key, inv, query_gain, key_gain)


def scaled(q_h, k_h, inv, qg, kg, qo_h, ko_h, q, k, qo, ko, in_sem, out_sem):
    chunks, _, part = q.shape[0], q.shape[1], q.shape[2]
    rows = q.shape[1]
    both = ((q_h, q, qg, qo, qo_h), (k_h, k, kg, ko, ko_h))
    loads, stores = [], []
    for c in range(chunks):
        for i, (src, buf, _, obuf, dst) in enumerate(both):
            at = pl.ds(c * rows, rows)
            loads.append(pltpu.make_async_copy(src.at[at], buf.at[c], in_sem.at[i, c]))
            stores.append(pltpu.make_async_copy(obuf.at[c], dst.at[at], out_sem.at[i, c]))
    for copy in loads:
        copy.start()
    for c in range(chunks):
        for i, (_, buf, gain, obuf, _) in enumerate(both):
            loads[2 * c + i].wait()
            factor = inv[pl.ds(c * rows, rows), pl.ds(i * 128, 128)]
            for n in range(0, part, 128):
                at = pl.ds(n, 128)
                obuf[c, :, at] = (buf[c, :, at].astype(F32) * factor * gain[at].reshape(1, 128)).astype(BF16)
            stores[2 * c + i].start()
    for copy in stores:
        copy.wait()


def finish(query, key, inv, query_gain, key_gain):
    tokens, part = query.shape
    chunks = tokens // 128
    out = jax.ShapeDtypeStruct((tokens, part), BF16)
    V, dma = pltpu.VMEM, pltpu.SemaphoreType.DMA
    return pl.pallas_call(
        scaled,
        out_shape=(out, out),
        in_specs=[pl.BlockSpec(memory_space=pl.ANY)] * 2 + [pl.BlockSpec(memory_space=V)] * 3,
        out_specs=(pl.BlockSpec(memory_space=pl.ANY),) * 2,
        scratch_shapes=[
            V((chunks, 128, part), BF16), V((chunks, 128, part), BF16), V((chunks, 128, part), BF16), V((chunks, 128, part), BF16),
            dma((2, chunks)), dma((2, chunks)),
        ],
        compiler_params=pltpu.CompilerParams(vmem_limit_bytes=67043328),
    )(query, key, inv, query_gain, key_gain)


def solution(mesh):
    in_specs = (
        P("tm", "rows", None, None), P(), P(), P(), P(), P(), P(), P(), P(), P(),
        P(None, "tm"), P("tm"), P("tm"), P(None, "tm"), P("tm"), P("tm"), P(),
    )
    out_specs = (P("rows", "tm"), P("rows", "tm"))
    return jax.shard_map(per_device, mesh=mesh, in_specs=in_specs, out_specs=out_specs, check_vma=False)
```
